512 devices in a mesh: section: 8 (over y_lo, x), fsdp: 64 (over y_hi, z, core).
Axes of the slice: x: 4, y: 4 (y_hi: 2, y_lo: 2; y = y_hi * 2 + y_lo), z: 16, core: 2. Of those that a mesh axis runs over, the one named last changes fastest.
Arguments:
- inputs: bfloat16 [8, 8, 128, 64, 256], P('section', None, 'fsdp'), may hold values from -6 to 6
- conv_first: bfloat16 [8, 27, 256, 256], P('section', None, 'fsdp'), may hold values from -0.078125 to 0.078125
- conv_second: bfloat16 [8, 27, 256, 256], P('section', None, 'fsdp'), may hold values from -0.078125 to 0.078125
- gain_first: float32 [8, 256], P('section'), may hold values from 0.5 to 2
- gain_second: float32 [8, 256], P('section'), may hold values from 0.5 to 2
- skip_weight: bfloat16 [4, 256, 256], P(None, 'fsdp'), may hold values from -0.375 to 0.375
Outputs:
- section_out: bfloat16 [8, 8, 128, 64, 256], P('section', None, 'fsdp')
The draws below stay inside these ranges and needn't reach their ends.
All inputs are finite; a program needn't handle non-finite values.
Results may differ from the reference program's by a relative error of at most 0.008.
Values may be sent and summed in bfloat16 or wider, within the bound.
A program may use at most 64 MiB of HBM per device.

```python
import math
import jax
import jax.numpy as jnp
from jax import lax

C = 256
DEPTH = 8
WIDE = 64
HEIGHT = 128
SECTIONS = 8
ENC = 4


def block_scale(rng, shape, cuts, low, high):
    factor_of = 1.0
    for position, shards_of in cuts:
        heights = jax.random.uniform(jax.random.fold_in(jax.random.fold_in(rng, 6), position), (shards_of,), jnp.float32, low / len(cuts), high / len(cuts))
        factor_of = factor_of * jnp.repeat(jnp.exp(heights), shape[position] // shards_of).reshape((-1,) + (1,) * (len(shape) - 1 - position))
    return factor_of


def bell_draw(key, dims, deviation, limit, cuts=(), held_as=jnp.bfloat16):
    level = block_scale(key, dims, cuts, -0.22, 0.18) if cuts else 1.0
    result = jax.random.normal(key, dims, jnp.float32) * deviation * level
    return jnp.minimum(jnp.maximum(result, -limit), limit).astype(held_as)


def setup_inputs(seed: int = 0) -> dict:
    splits = jax.random.split(jax.random.key(seed), 7)
    return {
        "inputs": bell_draw(splits[0], (SECTIONS, DEPTH, HEIGHT, WIDE, C), 1.0, 6.0, ((0, 8), (2, 64))),
        "conv_first": bell_draw(splits[1], (SECTIONS, 27, C, C), (27 * C) ** -0.5, 0.078125, ((0, 8), (2, 64))),
        "conv_second": bell_draw(splits[2], (SECTIONS, 27, C, C), (27 * C) ** -0.5, 0.078125, ((0, 8), (2, 64))),
        "gain_first": jnp.clip(jnp.exp(math.log(2.0) - 1.3862944 * jax.random.uniform(splits[3], (SECTIONS, C), jnp.float32) ** block_scale(splits[3], (SECTIONS, C), ((0, 8),), -0.2, 0.2)), 0.5, 2.0),
        "gain_second": jnp.clip(jnp.exp(math.log(2.0) - 1.3862944 * jax.random.uniform(splits[4], (SECTIONS, C), jnp.float32) ** block_scale(splits[4], (SECTIONS, C), ((0, 8),), -0.2, 0.2)), 0.5, 2.0),
        "skip_weight": bell_draw(splits[5], (ENC, C, C), C ** -0.5, 0.375, ((1, 64),)),
    }


def activated(values, gain_row):
    wide_values = values.astype(jnp.float32)
    scale = lax.rsqrt(lax.optimization_barrier(jnp.mean(wide_values * wide_values, axis=-1, keepdims=True)) + 1e-06)
    return jax.nn.silu(wide_values * scale * gain_row)

def conv_same(values, kernel):
    channels = values.shape[3]
    padded = jnp.pad(values, ((1, 1), (1, 1), (1, 1), (0, 0)))
    depth_n, rows_n, wide_n = (values.shape[0], values.shape[1], values.shape[2])
    running = jnp.zeros((depth_n * rows_n * wide_n, kernel.shape[2]), jnp.float32)
    for tap_index in range(27):
        off_depth, remainder = divmod(tap_index, 9)
        off_rows, off_wide = divmod(remainder, 3)
        window = padded[off_depth:off_depth + depth_n, off_rows:off_rows + rows_n, off_wide:off_wide + wide_n]
        running = running + jnp.dot(window.reshape(-1, channels), kernel[tap_index], preferred_element_type=jnp.float32)
    return running.reshape(depth_n, rows_n, wide_n, kernel.shape[2])

def reference(inputs, conv_first, conv_second, gain_first, gain_second, skip_weight):
    blocks = []
    for section_pos in range(SECTIONS):
        current = inputs[section_pos]
        first = activated(current, gain_first[section_pos]).astype(jnp.bfloat16)
        hidden = conv_same(first, conv_first[section_pos])
        second = activated(hidden, gain_second[section_pos]).astype(jnp.bfloat16)
        block = (current.astype(jnp.float32) + conv_same(second, conv_second[section_pos])).astype(jnp.bfloat16)
        blocks.append(block)
    results = []
    channels = inputs.shape[4]
    for section_pos in range(SECTIONS):
        if section_pos < ENC:
            results.append(blocks[section_pos])
        else:
            paired = blocks[section_pos - ENC]
            projection = jnp.dot(paired.reshape(-1, channels), skip_weight[section_pos - ENC], preferred_element_type=jnp.float32)
            joined = blocks[section_pos].astype(jnp.float32) + projection.reshape(paired.shape)
            results.append(joined.astype(jnp.bfloat16))
    return jnp.stack(results)
```

```python
import functools

import jax
import jax.numpy as jnp
import numpy as np
from jax import lax
from jax.experimental import pallas as pl
from jax.experimental.pallas import tpu as pltpu
from jax.sharding import PartitionSpec as P

MESH = pl.DeviceIdType.MESH
NZ = 16
RIGHT_STEPS = 8
LEFT_STEPS = 7
MIB = 1 << 20


def gather_kernel(ws_ref, g_ref, local_sem, pair_send, pair_recv, ring_send, ring_recv, core_send, core_recv):
    section = lax.axis_index("section")
    me = lax.axis_index("fsdp")
    h, z, c = me // 32, (me // 2) % NZ, me % 2

    def device(h_at, z_at, c_at):
        return (section, h_at * 32 + z_at * 2 + c_at)

    partner = device(1 - h, z, c)
    sibling = device(h, z, 1 - c)
    neighbours = (device(h, (z + 1) % NZ, c), device(h, (z + NZ - 1) % NZ, c))

    barrier = pltpu.get_barrier_semaphore()
    for other in (partner, sibling) + neighbours:
        pl.semaphore_signal(barrier, inc=1, device_id=other, device_id_type=MESH)
    pl.semaphore_wait(barrier, 4)

    def half(q):
        return h if q == 0 else 1 - h

    def origin(direction, step):
        return (z + NZ - step) % NZ if direction == 0 else (z + step) % NZ

    def remote(src, slot, to, send, recv):
        return pltpu.make_async_remote_copy(
            src_ref=src, dst_ref=slot, send_sem=send, recv_sem=recv, device_id=to, device_id_type=MESH
        )

    def pair_copy(k):
        return remote(ws_ref.at[k], g_ref.at[k, z, c, h], partner, pair_send.at[k], pair_recv.at[k])

    def pair_arrival(k):
        slot = g_ref.at[k, z, c, 1 - h]
        return remote(slot, slot, partner, pair_send.at[k], pair_recv.at[k])

    def ring_copy(k, q, direction, step):
        at = origin(direction, step - 1)
        slot = g_ref.at[k, at, c, half(q)]
        src = ws_ref.at[k] if step == 1 and q == 0 else slot
        sems = (k, q, direction, step - 1)
        return remote(src, slot, neighbours[direction], ring_send.at[sems], ring_recv.at[sems])

    def ring_arrival(k, q, direction, step):
        slot = g_ref.at[k, origin(direction, step), c, half(q)]
        sems = (k, q, direction, step - 1)
        return remote(slot, slot, neighbours[direction], ring_send.at[sems], ring_recv.at[sems])

    def core_index(direction, step):
        return step if direction == 0 else RIGHT_STEPS + step

    def core_copy(k, q, direction, step, own=False):
        at = origin(direction, step)
        slot = g_ref.at[k, at, c, half(q)]
        sems = (k, q, core_index(direction, step))
        return remote(ws_ref.at[k] if own else slot, slot, sibling, core_send.at[sems], core_recv.at[sems])

    def core_arrival(k, q, direction, step):
        slot = g_ref.at[k, origin(direction, step), 1 - c, half(q)]
        sems = (k, q, core_index(direction, step))
        return remote(slot, slot, sibling, core_send.at[sems], core_recv.at[sems])

    steps = (RIGHT_STEPS, LEFT_STEPS)

    def begin(k):
        for direction in (0, 1):
            ring_copy(k, 0, direction, 1).start()
        core_copy(k, 0, 0, 0, own=True).start()

    def begin_pair(k):
        pair_arrival(k).wait_recv()
        for direction in (0, 1):
            ring_copy(k, 1, direction, 1).start()
        core_copy(k, 1, 0, 0).start()

    for k in (0, 1):
        pair_copy(k).start()
    begin(0)
    local = [pltpu.make_async_copy(ws_ref.at[k], g_ref.at[k, z, c, h], local_sem.at[k]) for k in (0, 1)]
    for copy in local:
        copy.start()
    begin_pair(0)
    for k in (0, 1):
        for step in range(1, RIGHT_STEPS + 1):
            for q in (0, 1):
                for direction in (0, 1):
                    if step > steps[direction]:
                        continue
                    ring_arrival(k, q, direction, step).wait_recv()
                    if step < steps[direction]:
                        ring_copy(k, q, direction, step + 1).start()
                    core_copy(k, q, direction, step).start()
            if k == 0 and step == RIGHT_STEPS - 1:
                begin(1)
                begin_pair(1)
    for copy in local:
        copy.wait()
    for k in (0, 1):
        pair_copy(k).wait_send()
        for q in (0, 1):
            for direction in (0, 1):
                for step in range(1, steps[direction] + 1):
                    ring_copy(k, q, direction, step).wait_send()
                    core_copy(k, q, direction, step).wait_send()
                    core_arrival(k, q, direction, step).wait_recv()
            core_copy(k, q, 0, 0).wait_send()
            core_arrival(k, q, 0, 0).wait_recv()


def gathered(ws):
    return pl.pallas_call(
        gather_kernel,
        out_shape=jax.ShapeDtypeStruct((2, NZ, 2, 2, 7, 16, 256), jnp.bfloat16),
        in_specs=[pl.BlockSpec(memory_space=pltpu.VMEM)],
        out_specs=pl.BlockSpec(memory_space=pltpu.VMEM),
        scratch_shapes=[
            pltpu.SemaphoreType.DMA((2,)),
            pltpu.SemaphoreType.DMA((2,)),
            pltpu.SemaphoreType.DMA((2,)),
            pltpu.SemaphoreType.DMA((2, 2, 2, RIGHT_STEPS)),
            pltpu.SemaphoreType.DMA((2, 2, 2, RIGHT_STEPS)),
            pltpu.SemaphoreType.DMA((2, 2, NZ)),
            pltpu.SemaphoreType.DMA((2, 2, NZ)),
        ],
        compiler_params=pltpu.CompilerParams(collective_id=0, has_side_effects=True, vmem_limit_bytes=24 * MIB),
    )(ws)


def row_order():
    order = np.zeros((256, 256), np.float32)
    for tap in range(4):
        for h in range(2):
            for z in range(4):
                for c in range(2):
                    for i in range(4):
                        order[tap * 64 + h * 32 + z * 8 + c * 4 + i, z * 64 + c * 32 + h * 16 + tap * 4 + i] = 1.0
    return order


def activated(values, gain_row):
    wide_values = values.astype(jnp.float32)
    scale = lax.rsqrt(jnp.mean(wide_values * wide_values, axis=-1, keepdims=True) + 1e-06)
    return jax.nn.silu(wide_values * scale * gain_row)


def order_weights(g_ref, order_ref, w_ref):
    def ordered(group, carry):
        for zq in range(4):
            rows = g_ref[0, 4 * zq : 4 * zq + 4, :, :, group].reshape(256, 256)
            sorted_rows = jnp.dot(order_ref[...], rows, preferred_element_type=jnp.float32).astype(jnp.bfloat16)
            for tap in range(4):
                for h in range(2):
                    at = tap * 64 + h * 32
                    w_ref[4 * group + tap, h * 128 + zq * 32 : h * 128 + zq * 32 + 32, :] = sorted_rows[at : at + 32]
        return carry

    lax.fori_loop(0, 7, ordered, 0)


def conv_kernel(last, ext_ref, g_ref, order_ref, side_ref, out_ref, *rest):
    if last:
        skip_ref, w_ref, a_ref = rest
    else:
        w_ref, a_ref = rest
    order_weights(g_ref, order_ref, w_ref)
    for c in range(3):
        for d in (0, 9):
            a_ref[c, d] = jnp.zeros((4, 64, 256), jnp.bfloat16)
    place = lax.broadcasted_iota(jnp.int32, (64, 256), 0)

    def fill(d, carry):
        for r in range(4):
            plane = ext_ref[d, r]
            wide = plane.astype(jnp.float32)
            a_ref[1, d + 1, r] = plane
            a_ref[0, d + 1, r] = jnp.where(place == 0, 0.0, pltpu.roll(wide, 1, 0)).astype(jnp.bfloat16)
            a_ref[2, d + 1, r] = jnp.where(place == 63, 0.0, pltpu.roll(wide, 63, 0)).astype(jnp.bfloat16)
        return carry

    lax.fori_loop(0, 8, fill, 0)

    def chunk(m, carry):
        d = m * 2
        acc = jnp.zeros((256, 256), jnp.float32)
        for tap in range(27):
            off_depth, remainder = divmod(tap, 9)
            off_rows, off_wide = divmod(remainder, 3)
            window = a_ref[off_wide, pl.ds(d + off_depth, 2), off_rows : off_rows + 2]
            acc = acc + jnp.dot(window.reshape(256, 256), w_ref[tap], preferred_element_type=jnp.float32)
        if last:
            result = side_ref[pl.ds(d, 2)].reshape(256, 256).astype(jnp.float32) + acc
        else:
            scale = lax.rsqrt(jnp.mean(acc * acc, axis=-1, keepdims=True) + 1e-06)
            v = acc * scale * side_ref[...]
            result = v / (1.0 + jnp.exp(-v))
        out_ref[pl.ds(d, 2)] = result.astype(jnp.bfloat16).reshape(2, 2, 64, 256)
        return carry

    lax.fori_loop(0, 4, chunk, 0)
    if last:
        skip_ref[...] = w_ref[27]


def conv(last, k, ext, g, order, side):
    out_shape = [jax.ShapeDtypeStruct((8, 2, 64, 256), jnp.bfloat16)]
    if last:
        out_shape.append(jax.ShapeDtypeStruct((256, 256), jnp.bfloat16))
    whole = pl.BlockSpec(memory_space=pltpu.VMEM)
    zeros = (0,) * 6
    return pl.pallas_call(
        functools.partial(conv_kernel, last),
        grid=(1,),
        out_shape=out_shape,
        in_specs=[
            whole,
            pl.BlockSpec((1, NZ, 2, 2, 7, 16, 256), lambda i: (k,) + zeros),
            whole,
            whole,
        ],
        out_specs=[whole] * len(out_shape),
        scratch_shapes=[
            pltpu.VMEM((28, 256, 256), jnp.bfloat16),
            pltpu.VMEM((3, 10, 4, 64, 256), jnp.bfloat16),
        ],
        compiler_params=pltpu.CompilerParams(vmem_limit_bytes=48 * MIB),
    )(ext, g, order, side)


def with_halo(cells):
    head, tail = cells[:, :1], cells[:, 1:]
    count = lax.axis_size("fsdp")
    above = lax.ppermute(tail, "fsdp", [(i, i + 1) for i in range(count - 1)])
    below = lax.ppermute(head, "fsdp", [(i + 1, i) for i in range(count - 1)])
    return jnp.concatenate([above, cells, below], axis=1)


def shards(inputs, conv_first, conv_second, gain_first, gain_second, skip_weight):
    half_count = lax.axis_size("section") // 2
    decoder_pos = jnp.clip(lax.axis_index("section") - half_count, 0, half_count - 1)
    current = inputs[0]
    skip_rows = lax.dynamic_index_in_dim(skip_weight, decoder_pos, 0, keepdims=True)
    ws = jnp.stack(
        [
            jnp.concatenate([conv_first[0], jnp.zeros_like(skip_rows)], axis=0),
            jnp.concatenate([conv_second[0], skip_rows], axis=0),
        ]
    ).reshape(2, 7, 16, 256)
    g = gathered(ws)
    order = jnp.asarray(row_order(), jnp.bfloat16)
    first = activated(current, gain_first[0]).astype(jnp.bfloat16)
    (second,) = conv(False, 0, with_halo(first), g, order, gain_second)
    block, skip = conv(True, 1, with_halo(second), g, order, current)
    paired = lax.ppermute(block, "section", [(s, s + half_count) for s in range(half_count)])
    projection = jnp.dot(paired.reshape(-1, 256), skip, preferred_element_type=jnp.float32)
    return (block.astype(jnp.float32) + projection.reshape(block.shape)).astype(jnp.bfloat16)[None]


def solution(mesh):
    in_specs = (
        P("section", None, "fsdp", None, None),
        P("section", None, "fsdp", None),
        P("section", None, "fsdp", None),
        P("section", None),
        P("section", None),
        P(None, "fsdp", None),
    )
    out_specs = P("section", None, "fsdp", None, None)
    return jax.shard_map(shards, mesh=mesh, in_specs=in_specs, out_specs=out_specs, check_vma=False)
```

```python
import jax
import jax.numpy as jnp
import numpy as np
from jax import lax
from jax.experimental import pallas as pl
from jax.experimental.pallas import tpu as pltpu
from jax.sharding import PartitionSpec as P

MESH = pl.DeviceIdType.MESH
NZ = 16
RIGHT_STEPS = 8
LEFT_STEPS = 7
LAG = 0
CHUNKS = 4
MIB = 1 << 20


def row_order():
    order = np.zeros((256, 256), np.float32)
    for tap in range(4):
        for h in range(2):
            for z in range(4):
                for c in range(2):
                    for i in range(4):
                        order[tap * 64 + h * 32 + z * 8 + c * 4 + i, z * 64 + c * 32 + h * 16 + tap * 4 + i] = 1.0
    return order


def normed(values, gain_row):
    scale = lax.rsqrt(jnp.mean(values * values, axis=-1, keepdims=True) + 1e-06)
    v = values * scale * gain_row
    return (v / (1.0 + jnp.exp(-v))).astype(jnp.bfloat16)


def order_weights(g_ref, k, order_ref, w_ref):
    def ordered(group, carry):
        for zq in range(4):
            rows = g_ref[k, 4 * zq : 4 * zq + 4, :, :, group].reshape(256, 256)
            sorted_rows = jnp.dot(order_ref[...], rows, preferred_element_type=jnp.float32).astype(jnp.bfloat16)
            for tap in range(4):
                for h in range(2):
                    at = tap * 64 + h * 32
                    w_ref[4 * group + tap, h * 128 + zq * 32 : h * 128 + zq * 32 + 32, :] = sorted_rows[at : at + 32]
        return carry

    lax.fori_loop(0, 7, ordered, 0)


def put_plane(a_ref, d, r, plane):
    place = lax.broadcasted_iota(jnp.int32, (64, 256), 0)
    wide = plane.astype(jnp.float32)
    a_ref[1, d + 1, r] = plane
    a_ref[0, d + 1, r] = jnp.where(place == 0, 0.0, pltpu.roll(wide, 1, 0)).astype(jnp.bfloat16)
    a_ref[2, d + 1, r] = jnp.where(place == 63, 0.0, pltpu.roll(wide, 63, 0)).astype(jnp.bfloat16)


def taps(a_ref, w_ref, d):
    acc = jnp.zeros((256, 256), jnp.float32)
    for tap in range(27):
        off_depth, remainder = divmod(tap, 9)
        off_rows, off_wide = divmod(remainder, 3)
        window = a_ref[off_wide, pl.ds(d + off_depth, 2), off_rows : off_rows + 2]
        acc = acc + jnp.dot(window.reshape(256, 256), w_ref[tap], preferred_element_type=jnp.float32)
    return acc


def level_kernel(
    x_ref, ws_ref, order_ref, gain1_ref, gain2_ref, out_ref,
    g_ref, w_ref, a1_ref, a2_ref, f_ref, halo_ref, block_ref, skip_in_ref,
    local_sem, pair_send, pair_recv, ring_send, ring_recv, core_send, core_recv, halo_send, halo_recv, skip_send, skip_recv,
):
    section = lax.axis_index("section")
    me = lax.axis_index("fsdp")
    h, z, c = me // 32, (me // 2) % NZ, me % 2

    def device(h_at, z_at, c_at):
        return (section, h_at * 32 + z_at * 2 + c_at)

    partner = device(1 - h, z, c)
    sibling = device(h, z, 1 - c)
    neighbours = (device(h, (z + 1) % NZ, c), device(h, (z + NZ - 1) % NZ, c))
    above, below = (section, (me + 63) % 64), (section, (me + 1) % 64)
    paired = ((section + 4) % 8, me)

    barrier = pltpu.get_barrier_semaphore()
    for other in (partner, sibling, above, below, paired) + neighbours:
        pl.semaphore_signal(barrier, inc=1, device_id=other, device_id_type=MESH)
    pl.semaphore_wait(barrier, 7)

    def half(q):
        return h if q == 0 else 1 - h

    def origin(direction, step):
        return (z + NZ - step) % NZ if direction == 0 else (z + step) % NZ

    def remote(src, slot, to, send, recv):
        return pltpu.make_async_remote_copy(
            src_ref=src, dst_ref=slot, send_sem=send, recv_sem=recv, device_id=to, device_id_type=MESH
        )

    def pair_copy(k):
        return remote(ws_ref.at[k], g_ref.at[k, z, c, h], partner, pair_send.at[k], pair_recv.at[k])

    def pair_arrival(k):
        slot = g_ref.at[k, z, c, 1 - h]
        return remote(slot, slot, partner, pair_send.at[k], pair_recv.at[k])

    def ring_copy(k, q, direction, step):
        at = origin(direction, step - 1)
        slot = g_ref.at[k, at, c, half(q)]
        src = ws_ref.at[k] if step == 1 and q == 0 else slot
        sems = (k, q, direction, step - 1)
        return remote(src, slot, neighbours[direction], ring_send.at[sems], ring_recv.at[sems])

    def ring_arrival(k, q, direction, step):
        slot = g_ref.at[k, origin(direction, step), c, half(q)]
        sems = (k, q, direction, step - 1)
        return remote(slot, slot, neighbours[direction], ring_send.at[sems], ring_recv.at[sems])

    def core_index(direction, step):
        return step if direction == 0 else RIGHT_STEPS + step

    def core_copy(k, q, direction, step, own=False):
        slot = g_ref.at[k, origin(direction, step), c, half(q)]
        sems = (k, q, core_index(direction, step))
        return remote(ws_ref.at[k] if own else slot, slot, sibling, core_send.at[sems], core_recv.at[sems])

    def core_arrival(k, q, direction, step):
        slot = g_ref.at[k, origin(direction, step), 1 - c, half(q)]
        sems = (k, q, core_index(direction, step))
        return remote(slot, slot, sibling, core_send.at[sems], core_recv.at[sems])

    steps = (RIGHT_STEPS, LEFT_STEPS)

    def begin(k):
        for direction in (0, 1):
            ring_copy(k, 0, direction, 1).start()
        core_copy(k, 0, 0, 0, own=True).start()

    def begin_pair(k):
        pair_arrival(k).wait_recv()
        for direction in (0, 1):
            ring_copy(k, 1, direction, 1).start()
        core_copy(k, 1, 0, 0).start()

    def core_wait(k):
        for q in (0, 1):
            core_arrival(k, q, 0, 0).wait_recv()
            for direction in (0, 1):
                for step in range(1, steps[direction] + 1):
                    core_arrival(k, q, direction, step).wait_recv()

    def halo_copy(k, row, m):
        span = pl.ds(2 * m, 2)
        return remote(
            f_ref.at[k, span, row], halo_ref.at[k, 1 - row, span], above if row == 0 else below,
            halo_send.at[k, row, m], halo_recv.at[k, 1 - row, m],
        )

    def halo_arrival(k, side, m):
        slot = halo_ref.at[k, side, pl.ds(2 * m, 2)]
        return remote(slot, slot, above if side == 0 else below, halo_send.at[k, side, m], halo_recv.at[k, side, m])

    inner = (me > 0, me < 63)

    def halo_start(k, m):
        for row in (0, 1):
            @pl.when(inner[row])
            def _():
                halo_copy(k, row, m).start()

    def halo_sent(k):
        for row in (0, 1):
            @pl.when(inner[row])
            def _():
                for m in range(CHUNKS):
                    halo_copy(k, row, m).wait_send()

    def halo_fill(k, a_ref):
        for side in (0, 1):
            @pl.when(inner[side])
            def _():
                for m in range(CHUNKS):
                    halo_arrival(k, side, m).wait_recv()

            @pl.when(jnp.logical_not(inner[side]))
            def _():
                halo_ref[k, side] = jnp.zeros((8, 64, 256), jnp.bfloat16)

        def fill(d, carry):
            for side in (0, 1):
                put_plane(a_ref, d, 3 * side, halo_ref[k, side, d])
            return carry

        lax.fori_loop(0, 8, fill, 0)

    def activate(d, carry):
        values = normed(x_ref[d].reshape(128, 256).astype(jnp.float32), gain1_ref[...])
        for r in range(2):
            plane = values[64 * r : 64 * r + 64]
            f_ref[0, d, r] = plane
            put_plane(a1_ref, d, r + 1, plane)
        return carry

    def first_chunk(m):
        values = normed(taps(a1_ref, w_ref, 2 * m), gain2_ref[...])
        for dd in range(2):
            for r in range(2):
                at = (2 * dd + r) * 64
                f_ref[1, 2 * m + dd, r] = values[at : at + 64]
                put_plane(a2_ref, 2 * m + dd, r + 1, values[at : at + 64])
        halo_start(1, m)

    for k in (0, 1):
        pair_copy(k).start()
    begin(0)
    if LAG == 0:
        begin(1)
    local = [pltpu.make_async_copy(ws_ref.at[k], g_ref.at[k, z, c, h], local_sem.at[k]) for k in (0, 1)]
    for copy in local:
        copy.start()
    lax.fori_loop(0, 8, activate, 0)
    for m in range(CHUNKS):
        halo_start(0, m)
    begin_pair(0)
    if LAG == 0:
        begin_pair(1)
    for ref in (a1_ref, a2_ref):
        for off in range(3):
            for d in (0, 9):
                ref[off, d] = jnp.zeros((4, 64, 256), jnp.bfloat16)
    for index in range(1, RIGHT_STEPS + LAG + 1):
        for q in (0, 1):
            for k in (0, 1):
                step = index - LAG * k
                for direction in (0, 1):
                    if step < 1 or step > steps[direction]:
                        continue
                    ring_arrival(k, q, direction, step).wait_recv()
                    if step < steps[direction]:
                        ring_copy(k, q, direction, step + 1).start()
                    core_copy(k, q, direction, step).start()
        if index == LAG:
            begin(1)
            begin_pair(1)
        if index == 2:
            halo_fill(0, a1_ref)
        if index == RIGHT_STEPS + min(LAG, 1):
            local[0].wait()
            core_wait(0)
            order_weights(g_ref, 0, order_ref, w_ref)
        m = index - RIGHT_STEPS - 2
        if 0 <= m < CHUNKS:
            first_chunk(m)
    for m in range(max(0, LAG - 1), CHUNKS):
        first_chunk(m)
    local[1].wait()
    core_wait(1)
    order_weights(g_ref, 1, order_ref, w_ref)
    halo_fill(1, a2_ref)

    def skip_copy(m):
        span = pl.ds(2 * m, 2)
        return remote(block_ref.at[span], skip_in_ref.at[span], paired, skip_send.at[m], skip_recv.at[m])

    def second_chunk(m, carry):
        span = pl.ds(2 * m, 2)
        values = x_ref[span].reshape(256, 256).astype(jnp.float32) + taps(a2_ref, w_ref, 2 * m)
        values = values.astype(jnp.bfloat16).reshape(2, 2, 64, 256)
        block_ref[span] = values
        out_ref[span] = values

        @pl.when(section < 4)
        def _():
            skip_copy(m).start()

        return carry

    lax.fori_loop(0, CHUNKS, second_chunk, 0)

    @pl.when(section >= 4)
    def _():
        def join(m, carry):
            skip_copy(m).wait_recv()
            span = pl.ds(2 * m, 2)
            projection = jnp.dot(
                skip_in_ref[span].reshape(256, 256), w_ref[27], preferred_element_type=jnp.float32
            )
            joined = block_ref[span].reshape(256, 256).astype(jnp.float32) + projection
            out_ref[span] = joined.astype(jnp.bfloat16).reshape(2, 2, 64, 256)
            return carry

        lax.fori_loop(0, CHUNKS, join, 0)

    @pl.when(section < 4)
    def _():
        for m in range(CHUNKS):
            skip_copy(m).wait_send()

    for k in (0, 1):
        halo_sent(k)
        pair_copy(k).wait_send()
        for q in (0, 1):
            core_copy(k, q, 0, 0).wait_send()
            for direction in (0, 1):
                for step in range(1, steps[direction] + 1):
                    ring_copy(k, q, direction, step).wait_send()
                    core_copy(k, q, direction, step).wait_send()


def level(x, ws, order, gain1, gain2):
    whole = pl.BlockSpec(memory_space=pltpu.VMEM)
    dma = pltpu.SemaphoreType.DMA
    return pl.pallas_call(
        level_kernel,
        out_shape=jax.ShapeDtypeStruct((8, 2, 64, 256), jnp.bfloat16),
        in_specs=[whole] * 5,
        out_specs=whole,
        scratch_shapes=[
            pltpu.VMEM((2, NZ, 2, 2, 7, 16, 256), jnp.bfloat16),
            pltpu.VMEM((28, 256, 256), jnp.bfloat16),
            pltpu.VMEM((3, 10, 4, 64, 256), jnp.bfloat16),
            pltpu.VMEM((3, 10, 4, 64, 256), jnp.bfloat16),
            pltpu.VMEM((2, 8, 2, 64, 256), jnp.bfloat16),
            pltpu.VMEM((2, 2, 8, 64, 256), jnp.bfloat16),
            pltpu.VMEM((8, 2, 64, 256), jnp.bfloat16),
            pltpu.VMEM((8, 2, 64, 256), jnp.bfloat16),
            dma((2,)),
            dma((2,)),
            dma((2,)),
            dma((2, 2, 2, RIGHT_STEPS)),
            dma((2, 2, 2, RIGHT_STEPS)),
            dma((2, 2, NZ)),
            dma((2, 2, NZ)),
            dma((2, 2, CHUNKS)),
            dma((2, 2, CHUNKS)),
            dma((CHUNKS,)),
            dma((CHUNKS,)),
        ],
        compiler_params=pltpu.CompilerParams(collective_id=0, has_side_effects=True, vmem_limit_bytes=48 * MIB),
    )(x, ws, order, gain1, gain2)


def shards(inputs, conv_first, conv_second, gain_first, gain_second, skip_weight):
    half_count = lax.axis_size("section") // 2
    decoder_pos = jnp.clip(lax.axis_index("section") - half_count, 0, half_count - 1)
    skip_rows = lax.dynamic_index_in_dim(skip_weight, decoder_pos, 0, keepdims=True)
    ws = jnp.stack(
        [
            jnp.concatenate([conv_first[0], jnp.zeros_like(skip_rows)], axis=0),
            jnp.concatenate([conv_second[0], skip_rows], axis=0),
        ]
    ).reshape(2, 7, 16, 256)
    order = jnp.asarray(row_order(), jnp.bfloat16)
    return level(inputs[0], ws, order, gain_first, gain_second)[None]


def solution(mesh):
    in_specs = (
        P("section", None, "fsdp", None, None),
        P("section", None, "fsdp", None),
        P("section", None, "fsdp", None),
        P("section", None),
        P("section", None),
        P(None, "fsdp", None),
    )
    out_specs = P("section", None, "fsdp", None, None)
    return jax.shard_map(shards, mesh=mesh, in_specs=in_specs, out_specs=out_specs, check_vma=False)
```

```python
import jax
import jax.numpy as jnp
import numpy as np
from jax import lax
from jax.experimental import pallas as pl
from jax.experimental.pallas import tpu as pltpu
from jax.sharding import PartitionSpec as P

MESH = pl.DeviceIdType.MESH
NZ = 16
STEPS = ((8, 7), (7, 8))
CROSS = ()
CHUNKS = 4
MIB = 1 << 20


def row_order():
    order = np.zeros((256, 256), np.float32)
    for tap in range(4):
        for h in range(2):
            for z in range(4):
                for c in range(2):
                    for i in range(4):
                        order[tap * 64 + h * 32 + z * 8 + c * 4 + i, z * 64 + c * 32 + h * 16 + tap * 4 + i] = 1.0
    return order


def normed(values, gain_row):
    scale = lax.rsqrt(jnp.mean(values * values, axis=-1, keepdims=True) + 1e-06)
    v = values * scale * gain_row
    return (v / (1.0 + jnp.exp(-v))).astype(jnp.bfloat16)


def order_weights(g_ref, k, order_ref, w_ref):
    def ordered(group, carry):
        for zq in range(4):
            rows = g_ref[k, 4 * zq : 4 * zq + 4, :, :, group].reshape(256, 256)
            sorted_rows = jnp.dot(order_ref[...], rows, preferred_element_type=jnp.float32).astype(jnp.bfloat16)
            for tap in range(4):
                for h in range(2):
                    at = tap * 64 + h * 32
                    w_ref[4 * group + tap, h * 128 + zq * 32 : h * 128 + zq * 32 + 32, :] = sorted_rows[at : at + 32]
        return carry

    lax.fori_loop(0, 7, ordered, 0)


def put_plane(a_ref, d, r, plane):
    place = lax.broadcasted_iota(jnp.int32, (64, 256), 0)
    wide = plane.astype(jnp.float32)
    a_ref[1, d + 1, r] = plane
    a_ref[0, d + 1, r] = jnp.where(place == 0, 0.0, pltpu.roll(wide, 1, 0)).astype(jnp.bfloat16)
    a_ref[2, d + 1, r] = jnp.where(place == 63, 0.0, pltpu.roll(wide, 63, 0)).astype(jnp.bfloat16)


def taps(a_ref, w_ref, d):
    acc = jnp.zeros((256, 256), jnp.float32)
    for tap in range(27):
        off_depth, remainder = divmod(tap, 9)
        off_rows, off_wide = divmod(remainder, 3)
        window = a_ref[off_wide, pl.ds(d + off_depth, 2), off_rows : off_rows + 2]
        acc = acc + jnp.dot(window.reshape(256, 256), w_ref[tap], preferred_element_type=jnp.float32)
    return acc


def level_kernel(
    x_ref, ws_ref, order_ref, gain1_ref, gain2_ref, out_ref,
    g_ref, w_ref, a1_ref, a2_ref, f_ref, halo_ref, block_ref, skip_in_ref,
    local_sem, pair_send, pair_recv, cross_send, cross_recv, ring_send, ring_recv, core_send, core_recv, halo_send, halo_recv, skip_send, skip_recv,
):
    section = lax.axis_index("section")
    me = lax.axis_index("fsdp")
    h, z, c = me // 32, (me // 2) % NZ, me % 2

    def device(h_at, z_at, c_at):
        return (section, h_at * 32 + z_at * 2 + c_at)

    partner = device(1 - h, z, c)
    sibling = device(h, z, 1 - c)
    neighbours = (device(h, (z + 1) % NZ, c), device(h, (z + NZ - 1) % NZ, c))
    above, below = (section, (me + 63) % 64), (section, (me + 1) % 64)
    paired = ((section + 4) % 8, me)

    barrier = pltpu.get_barrier_semaphore()
    for other in (partner, sibling, above, below, paired) + neighbours:
        pl.semaphore_signal(barrier, inc=1, device_id=other, device_id_type=MESH)

    def activate(d, carry):
        values = normed(x_ref[d].reshape(128, 256).astype(jnp.float32), gain1_ref[...])
        for r in range(2):
            plane = values[64 * r : 64 * r + 64]
            f_ref[0, d, r] = plane
            put_plane(a1_ref, d, r + 1, plane)
        return carry

    lax.fori_loop(0, 8, activate, 0)
    for ref in (a1_ref, a2_ref):
        for off in range(3):
            for d in (0, 9):
                ref[off, d] = jnp.zeros((4, 64, 256), jnp.bfloat16)
    pl.semaphore_wait(barrier, 7)

    def half(q):
        return h if q == 0 else 1 - h

    def origin(direction, step):
        return (z + NZ - step) % NZ if direction == 0 else (z + step) % NZ

    def remote(src, slot, to, send, recv):
        return pltpu.make_async_remote_copy(
            src_ref=src, dst_ref=slot, send_sem=send, recv_sem=recv, device_id=to, device_id_type=MESH
        )

    def pair_copy(k):
        return remote(ws_ref.at[k], g_ref.at[k, z, c, h], partner, pair_send.at[k], pair_recv.at[k])

    def pair_arrival(k):
        slot = g_ref.at[k, z, c, 1 - h]
        return remote(slot, slot, partner, pair_send.at[k], pair_recv.at[k])

    def ring_copy(k, q, direction, step):
        at = origin(direction, step - 1)
        slot = g_ref.at[k, at, c, half(q)]
        src = ws_ref.at[k] if step == 1 and q == 0 else slot
        sems = (k, q, direction, step - 1)
        return remote(src, slot, neighbours[direction], ring_send.at[sems], ring_recv.at[sems])

    def ring_arrival(k, q, direction, step):
        slot = g_ref.at[k, origin(direction, step), c, half(q)]
        sems = (k, q, direction, step - 1)
        return remote(slot, slot, neighbours[direction], ring_send.at[sems], ring_recv.at[sems])

    def cross_copy(k, direction, step):
        slot = g_ref.at[k, origin(direction, step), c, h]
        sems = (k, direction, step - 1)
        return remote(slot, slot, partner, cross_send.at[sems], cross_recv.at[sems])

    def cross_arrival(k, direction, step):
        slot = g_ref.at[k, origin(direction, step), c, 1 - h]
        sems = (k, direction, step - 1)
        return remote(slot, slot, partner, cross_send.at[sems], cross_recv.at[sems])

    def crosses(q, step):
        return q == 1 and step in CROSS

    def core_index(direction, step):
        return step if direction == 0 else NZ - step

    def core_copy(k, q, direction, step, own=False):
        slot = g_ref.at[k, origin(direction, step), c, half(q)]
        sems = (k, q, core_index(direction, step))
        return remote(ws_ref.at[k] if own else slot, slot, sibling, core_send.at[sems], core_recv.at[sems])

    def core_arrival(k, q, direction, step):
        slot = g_ref.at[k, origin(direction, step), 1 - c, half(q)]
        sems = (k, q, core_index(direction, step))
        return remote(slot, slot, sibling, core_send.at[sems], core_recv.at[sems])

    def begin(k):
        for direction in (0, 1):
            ring_copy(k, 0, direction, 1).start()
        core_copy(k, 0, 0, 0, own=True).start()

    def begin_pair(k):
        pair_arrival(k).wait_recv()
        for direction in (0, 1):
            ring_copy(k, 1, direction, 1).start()
        core_copy(k, 1, 0, 0).start()

    def core_wait(k):
        for q in (0, 1):
            core_arrival(k, q, 0, 0).wait_recv()
            for direction in (0, 1):
                for step in range(1, STEPS[q][direction] + 1):
                    core_arrival(k, q, direction, step).wait_recv()

    def halo_copy(k, row, m):
        span = pl.ds(2 * m, 2)
        return remote(
            f_ref.at[k, span, row], halo_ref.at[k, 1 - row, span], above if row == 0 else below,
            halo_send.at[k, row, m], halo_recv.at[k, 1 - row, m],
        )

    def halo_arrival(k, side, m):
        slot = halo_ref.at[k, side, pl.ds(2 * m, 2)]
        return remote(slot, slot, above if side == 0 else below, halo_send.at[k, side, m], halo_recv.at[k, side, m])

    inner = (me > 0, me < 63)

    def halo_start(k, m):
        for row in (0, 1):
            @pl.when(inner[row])
            def _():
                halo_copy(k, row, m).start()

    def halo_sent(k):
        for row in (0, 1):
            @pl.when(inner[row])
            def _():
                for m in range(CHUNKS):
                    halo_copy(k, row, m).wait_send()

    def halo_fill(k, a_ref):
        for side in (0, 1):
            @pl.when(inner[side])
            def _():
                for m in range(CHUNKS):
                    halo_arrival(k, side, m).wait_recv()

            @pl.when(jnp.logical_not(inner[side]))
            def _():
                halo_ref[k, side] = jnp.zeros((8, 64, 256), jnp.bfloat16)

        def fill(d, carry):
            for side in (0, 1):
                put_plane(a_ref, d, 3 * side, halo_ref[k, side, d])
            return carry

        lax.fori_loop(0, 8, fill, 0)

    def first_chunk(m):
        values = normed(taps(a1_ref, w_ref, 2 * m), gain2_ref[...])
        for dd in range(2):
            for r in range(2):
                at = (2 * dd + r) * 64
                f_ref[1, 2 * m + dd, r] = values[at : at + 64]
                put_plane(a2_ref, 2 * m + dd, r + 1, values[at : at + 64])
        halo_start(1, m)

    for k in (0, 1):
        pair_copy(k).start()
        begin(k)
    local = [pltpu.make_async_copy(ws_ref.at[k], g_ref.at[k, z, c, h], local_sem.at[k]) for k in (0, 1)]
    for copy in local:
        copy.start()
    for m in range(CHUNKS):
        halo_start(0, m)
    for k in (0, 1):
        begin_pair(k)
    for step in range(1, NZ // 2 + 1):
        for q in (0, 1):
            for k in (0, 1):
                for direction in (0, 1):
                    if step > STEPS[q][direction]:
                        continue
                    if crosses(q, step):
                        cross_arrival(k, direction, step).wait_recv()
                    else:
                        ring_arrival(k, q, direction, step).wait_recv()
                    if step < STEPS[q][direction] and not crosses(q, step + 1):
                        ring_copy(k, q, direction, step + 1).start()
                    if q == 0 and step in CROSS:
                        cross_copy(k, direction, step).start()
                    core_copy(k, q, direction, step).start()
        if step == 2:
            halo_fill(0, a1_ref)
    local[0].wait()
    core_wait(0)
    order_weights(g_ref, 0, order_ref, w_ref)
    for m in range(CHUNKS):
        first_chunk(m)
    local[1].wait()
    core_wait(1)
    order_weights(g_ref, 1, order_ref, w_ref)
    halo_fill(1, a2_ref)

    def skip_copy(m):
        span = pl.ds(2 * m, 2)
        return remote(block_ref.at[span], skip_in_ref.at[span], paired, skip_send.at[m], skip_recv.at[m])

    def second_chunk(m, carry):
        span = pl.ds(2 * m, 2)
        values = x_ref[span].reshape(256, 256).astype(jnp.float32) + taps(a2_ref, w_ref, 2 * m)
        values = values.astype(jnp.bfloat16).reshape(2, 2, 64, 256)
        block_ref[span] = values
        out_ref[span] = values

        @pl.when(section < 4)
        def _():
            skip_copy(m).start()

        return carry

    lax.fori_loop(0, CHUNKS, second_chunk, 0)

    @pl.when(section >= 4)
    def _():
        def join(m, carry):
            skip_copy(m).wait_recv()
            span = pl.ds(2 * m, 2)
            projection = jnp.dot(
                skip_in_ref[span].reshape(256, 256), w_ref[27], preferred_element_type=jnp.float32
            )
            joined = block_ref[span].reshape(256, 256).astype(jnp.float32) + projection
            out_ref[span] = joined.astype(jnp.bfloat16).reshape(2, 2, 64, 256)
            return carry

        lax.fori_loop(0, CHUNKS, join, 0)

    @pl.when(section < 4)
    def _():
        for m in range(CHUNKS):
            skip_copy(m).wait_send()

    for k in (0, 1):
        halo_sent(k)
        pair_copy(k).wait_send()
        for q in (0, 1):
            core_copy(k, q, 0, 0).wait_send()
            for direction in (0, 1):
                for step in range(1, STEPS[q][direction] + 1):
                    core_copy(k, q, direction, step).wait_send()
                    if not crosses(q, step):
                        ring_copy(k, q, direction, step).wait_send()
                    if crosses(q, step):
                        cross_copy(k, direction, step).wait_send()


def level(x, ws, order, gain1, gain2):
    whole = pl.BlockSpec(memory_space=pltpu.VMEM)
    dma = pltpu.SemaphoreType.DMA
    return pl.pallas_call(
        level_kernel,
        out_shape=jax.ShapeDtypeStruct((8, 2, 64, 256), jnp.bfloat16),
        in_specs=[whole] * 5,
        out_specs=whole,
        scratch_shapes=[
            pltpu.VMEM((2, NZ, 2, 2, 7, 16, 256), jnp.bfloat16),
            pltpu.VMEM((28, 256, 256), jnp.bfloat16),
            pltpu.VMEM((3, 10, 4, 64, 256), jnp.bfloat16),
            pltpu.VMEM((3, 10, 4, 64, 256), jnp.bfloat16),
            pltpu.VMEM((2, 8, 2, 64, 256), jnp.bfloat16),
            pltpu.VMEM((2, 2, 8, 64, 256), jnp.bfloat16),
            pltpu.VMEM((8, 2, 64, 256), jnp.bfloat16),
            pltpu.VMEM((8, 2, 64, 256), jnp.bfloat16),
            dma((2,)),
            dma((2,)),
            dma((2,)),
            dma((2, 2, 8)),
            dma((2, 2, 8)),
            dma((2, 2, 2, 8)),
            dma((2, 2, 2, 8)),
            dma((2, 2, NZ)),
            dma((2, 2, NZ)),
            dma((2, 2, CHUNKS)),
            dma((2, 2, CHUNKS)),
            dma((CHUNKS,)),
            dma((CHUNKS,)),
        ],
        compiler_params=pltpu.CompilerParams(collective_id=0, has_side_effects=True, vmem_limit_bytes=48 * MIB),
    )(x, ws, order, gain1, gain2)


def shards(inputs, conv_first, conv_second, gain_first, gain_second, skip_weight):
    half_count = lax.axis_size("section") // 2
    decoder_pos = jnp.clip(lax.axis_index("section") - half_count, 0, half_count - 1)
    skip_rows = lax.dynamic_index_in_dim(skip_weight, decoder_pos, 0, keepdims=True)
    ws = jnp.stack(
        [
            jnp.concatenate([conv_first[0], jnp.zeros_like(skip_rows)], axis=0),
            jnp.concatenate([conv_second[0], skip_rows], axis=0),
        ]
    ).reshape(2, 7, 16, 256)
    order = jnp.asarray(row_order(), jnp.bfloat16)
    return level(inputs[0], ws, order, gain_first, gain_second)[None]


def solution(mesh):
    in_specs = (
        P("section", None, "fsdp", None, None),
        P("section", None, "fsdp", None),
        P("section", None, "fsdp", None),
        P("section", None),
        P("section", None),
        P(None, "fsdp", None),
    )
    out_specs = P("section", None, "fsdp", None, None)
    return jax.shard_map(shards, mesh=mesh, in_specs=in_specs, out_specs=out_specs, check_vma=False)
```
